256 devices in a mesh: seq: 32 (over x, z_lo, core), chan: 8 (over y, z_hi).
Axes of the slice: x: 4, y: 4, z: 8 (z_hi: 2, z_lo: 4; z = z_hi * 4 + z_lo), core: 2. Of those that a mesh axis runs over, the one named last changes fastest.
Arguments:
- values: bfloat16 [65536, 1024], P('seq', 'chan'), may hold values from -6 to 6
- inner_gate: bfloat16 [65536, 1024], P('seq', 'chan'), may hold values from -6 to 6
- outer_gate: bfloat16 [65536, 1024], P('seq', 'chan'), may hold values from -6 to 6
- filters: bfloat16 [65536, 64], P('seq', 'chan'), may hold values from -1.1 to 1.1
- skip: float32 [1024], P('chan'), may hold values from -4 to 4
- w_out: bfloat16 [1024, 1024], replicated, may hold values from -0.1875 to 0.1875
Outputs:
- mixed: bfloat16 [65536, 1024], P('seq', 'chan')
The draws below stay inside these ranges and needn't reach their ends.
All inputs are finite; a program needn't handle non-finite values.
Results may differ from the reference program's by a relative error of at most 0.006.
Values may be sent and summed in bfloat16 or wider, within the bound.
A program may use at most 128 MiB of HBM per device.

```python
import math
import jax
import jax.numpy as jnp
from jax import lax

D = 1024
GROUP = 16
TOKENS = 65536
GROUPS = 64


def draw_filters(key, part):
    keys = jax.random.split(key, 6)
    positions = jnp.arange(TOKENS, dtype=jnp.float32)[:, None]
    noise = jnp.clip(jax.random.normal(keys[0], (TOKENS, GROUPS), jnp.float32), -4.0, 4.0)
    slow_share = 0.5
    slow = jax.random.uniform(keys[1], (GROUPS,), jnp.float32) < slow_share
    slow_rate = jnp.exp(jax.random.uniform(keys[2], (GROUPS,), jnp.float32, math.log(0.02), math.log(0.3))) / TOKENS
    fast_rate = jnp.exp(jax.random.uniform(keys[3], (GROUPS,), jnp.float32, math.log(1.0 / 50.0), math.log(1.0 / 30.0)))
    decay_rate = jnp.where(slow, slow_rate, fast_rate)
    places = jax.random.randint(keys[4], (2, GROUPS), 0, TOKENS)
    drops = jax.random.uniform(keys[5], (2, GROUPS), jnp.float32, 0.5, 0.8)
    envelope = jnp.exp(-decay_rate[None, :] * positions)
    envelope = envelope * jnp.where(positions >= places[0][None, :].astype(jnp.float32), drops[0][None, :], 1.0)
    envelope = envelope * jnp.where(positions >= places[1][None, :].astype(jnp.float32), drops[1][None, :], 1.0)
    scaling = jnp.sqrt(2.0 * decay_rate / (1.0 - jnp.exp(-2.0 * decay_rate * TOKENS)))
    return (noise * envelope * scaling[None, :]).astype(jnp.bfloat16)


def shard_levels(key, extent, pieces, low, high):
    def one(dim, shards_of):
        draws = jax.random.uniform(jax.random.fold_in(jax.random.fold_in(key, 6), dim), (shards_of,), jnp.float32, low / len(pieces), high / len(pieces))
        return jnp.repeat(jnp.exp(draws), extent[dim] // shards_of).reshape((-1,) + (1,) * (len(extent) - dim - 1))

    factor_of = one(*pieces[0])
    for cut in pieces[1:]:
        factor_of = factor_of * one(*cut)
    return factor_of


def gaussian(stream_key, shape, deviation, reach, pieces=(), held_as=jnp.bfloat16):
    array = deviation * jax.random.normal(stream_key, shape, jnp.float32)
    if pieces:
        array = array * shard_levels(stream_key, shape, pieces, -0.22, 0.18)
    return jnp.clip(array, -reach, reach).astype(held_as)


def setup_inputs(seed: int = 0) -> dict:
    seeds = jax.random.split(jax.random.key(seed), 7)
    values = gaussian(seeds[0], (TOKENS, D), 1.0, 6.0, ((0, 32), (1, 8)))
    inner_gate = gaussian(seeds[1], (TOKENS, D), 1.0, 6.0, ((0, 32), (1, 8)))
    outer_gate = gaussian(seeds[2], (TOKENS, D), 1.0, 6.0, ((0, 32), (1, 8)))
    filters = draw_filters(jax.random.fold_in(seeds[6], 71), 0)
    skip = gaussian(seeds[4], (D,), 1.0, 4.0, ((0, 8),), jnp.float32)
    w_out = gaussian(seeds[5], (D, D), D ** -0.5, 0.1875)
    return dict(values=values, inner_gate=inner_gate, outer_gate=outer_gate, filters=filters, skip=skip, w_out=w_out)


def reference(values, inner_gate, outer_gate, filters, skip, w_out):
    signal = (inner_gate.astype(jnp.float32) * values.astype(jnp.float32)).astype(jnp.bfloat16)
    length = signal.shape[0]
    grouped = signal.astype(jnp.float32).reshape(length, GROUPS, GROUP).transpose(1, 0, 2)
    kernels = filters.astype(jnp.float32).T

    def one_group(pair):
        block, kernel = pair
        spectrum = jnp.fft.rfft(block, n=2 * length, axis=0) * jnp.fft.rfft(kernel, n=2 * length)[:, None]
        return jnp.fft.irfft(spectrum, n=2 * length, axis=0)[:length]

    conv = lax.map(one_group, (grouped, kernels))
    conv = conv.transpose(1, 0, 2).reshape(length, D).astype(jnp.bfloat16)
    gated = (outer_gate.astype(jnp.float32) * (conv.astype(jnp.float32) + skip[None, :] * signal.astype(jnp.float32))).astype(jnp.bfloat16)
    return jnp.dot(gated, w_out, preferred_element_type=jnp.float32).astype(jnp.bfloat16)
```

```python
import functools

import jax
import jax.numpy as jnp
import numpy as np
from jax import lax
from jax.experimental import pallas as pl
from jax.experimental.pallas import tpu as pltpu
from jax.sharding import PartitionSpec as P

F32 = jnp.float32
BF16 = jnp.bfloat16
LANES = 128
ROWS = 512
CHUNK = 256


def split_table(table):
    high = table.astype(jnp.bfloat16)
    low = (table - high.astype(np.float64)).astype(jnp.bfloat16)
    return high, low


@functools.lru_cache(maxsize=None)
def tables(rows):
    n = rows * LANES
    quarter = 4 * np.arange(rows, dtype=np.int64) + 1
    first = np.arange(rows, dtype=np.int64)
    angle = 2.0 * np.pi * ((quarter[:, None] * first[None, :]) % (4 * rows)) / (4 * rows)
    front = np.concatenate([np.cos(angle), -np.sin(angle)], axis=0)
    lane = np.arange(LANES, dtype=np.int64)
    angle = 2.0 * np.pi * (quarter[:, None] * lane[None, :]) / (4 * n)
    twist_real = np.cos(angle).astype(np.float32)
    twist_imag = (-np.sin(angle)).astype(np.float32)
    angle = 2.0 * np.pi * ((lane[:, None] * lane[None, :]) % LANES) / LANES
    cos, sin = np.cos(angle), np.sin(angle)
    mid = np.block([[cos, -sin], [sin, cos]])
    back = np.block([[cos, sin], [-sin, cos]])
    return (
        *split_table(front),
        *split_table(front.T / n),
        *split_table(mid),
        *split_table(back),
        twist_real,
        twist_imag,
    )


def halves(value):
    high = value.astype(BF16)
    return high, (value - high.astype(F32)).astype(BF16)


def dot(left, right):
    return jnp.dot(left, right, preferred_element_type=F32)


def dot3(left, right_high, right_low):
    left_high, left_low = halves(left)
    return dot(left_high, right_high) + (dot(left_high, right_low) + dot(left_low, right_high))


def pack_kernel(values_ref, inner_ref, filters_ref, out_ref, wide_ref, wide_filter_ref):
    parts = out_ref.shape[0]
    tiles = values_ref.shape[0] // LANES
    channels = values_ref.shape[1]
    groups = filters_ref.shape[1]
    for tile in range(tiles):
        rows = pl.ds(tile * LANES, LANES)
        signal = inner_ref[rows, :].astype(F32) * values_ref[rows, :].astype(F32)
        wide_ref[pl.ds(tile, channels, stride=tiles), :] = signal.T
        wide_filter_ref[pl.ds(tile, groups, stride=tiles), :] = filters_ref[rows, :].astype(F32).T
    own = channels // parts * tiles
    out_ref[:, :own, :] = wide_ref[...].astype(BF16).reshape(parts, own, LANES)
    for part in range(parts):
        group = part * groups // parts
        out_ref[part, own:, :] = wide_filter_ref[pl.ds(group * tiles, tiles), :].astype(BF16)


def conv_kernel(
    moved_ref,
    front_high,
    front_low,
    rear_high,
    rear_low,
    mid_high,
    mid_low,
    back_high,
    back_low,
    twist_real,
    twist_imag,
    out_ref,
    data_ref,
    filter_ref,
    high_ref,
    low_ref,
):
    parts, packed, _ = moved_ref.shape
    tiles = ROWS // parts
    count = packed // tiles - 1
    for part in range(parts):
        rows = pl.ds(part * tiles, tiles)
        for channel in range(count):
            data_ref[rows, pl.ds(channel * LANES, LANES)] = moved_ref[
                part, pl.ds(channel * tiles, tiles), :
            ]
        filter_ref[rows, :] = moved_ref[part, pl.ds(count * tiles, tiles), :]

    def forward(columns, rows):
        return dot(front_high[rows, :], columns) + dot(front_low[rows, :], columns)

    def chunk_step(step, carry):
        start = pl.multiple_of(step * CHUNK, CHUNK)
        real_rows = pl.ds(start, CHUNK)
        imag_rows = pl.ds(pl.multiple_of(start + ROWS, CHUNK), CHUNK)
        turn_real, turn_imag = twist_real[real_rows, :], twist_imag[real_rows, :]

        def spectrum(real, imag):
            turned = jnp.concatenate(
                [real * turn_real - imag * turn_imag, real * turn_imag + imag * turn_real], axis=1
            )
            both = dot3(turned, mid_high[...], mid_low[...])
            return both[:, :LANES], both[:, LANES:]

        kernel = filter_ref[...]
        kernel_real, kernel_imag = spectrum(forward(kernel, real_rows), forward(kernel, imag_rows))
        data = data_ref[...]
        all_real, all_imag = forward(data, real_rows), forward(data, imag_rows)
        for channel in range(count):
            lanes = pl.ds(channel * LANES, LANES)
            real, imag = spectrum(
                all_real[:, channel * LANES : (channel + 1) * LANES],
                all_imag[:, channel * LANES : (channel + 1) * LANES],
            )
            product = jnp.concatenate(
                [
                    real * kernel_real - imag * kernel_imag,
                    real * kernel_imag + imag * kernel_real,
                ],
                axis=1,
            )
            both = dot3(product, back_high[...], back_low[...])
            real, imag = both[:, :LANES], both[:, LANES:]
            high, low = halves(real * turn_real + imag * turn_imag)
            high_ref[real_rows, lanes], low_ref[real_rows, lanes] = high, low
            high, low = halves(imag * turn_real - real * turn_imag)
            high_ref[imag_rows, lanes], low_ref[imag_rows, lanes] = high, low
        return carry

    lax.fori_loop(0, ROWS // CHUNK, chunk_step, 0)

    def rear_step(step, carry):
        rows = pl.ds(pl.multiple_of(step * CHUNK, CHUNK), CHUNK)
        high, low = high_ref[...], low_ref[...]
        result = dot(rear_high[rows, :], high) + (
            dot(rear_low[rows, :], high) + dot(rear_high[rows, :], low)
        )
        result = result.astype(BF16)
        own = CHUNK // tiles
        for channel in range(count):
            out_ref[pl.ds(step * own, own), pl.ds(channel * tiles, tiles), :] = result[
                :, channel * LANES : (channel + 1) * LANES
            ].reshape(own, tiles, LANES)
        return carry

    lax.fori_loop(0, ROWS // CHUNK, rear_step, 0)


def gate_kernel(moved_ref, values_ref, inner_ref, outer_ref, skip_ref, out_ref, wide_ref):
    tiles = values_ref.shape[0] // LANES
    channels = values_ref.shape[1]
    wide_ref[...] = moved_ref[...].astype(F32).reshape(wide_ref.shape)
    for tile in range(tiles):
        rows = pl.ds(tile * LANES, LANES)
        conv = wide_ref[pl.ds(tile, channels, stride=tiles), :].T
        signal = inner_ref[rows, :].astype(F32) * values_ref[rows, :].astype(F32)
        signal = signal.astype(BF16).astype(F32)
        gated = outer_ref[rows, :].astype(F32) * (conv + skip_ref[...] * signal)
        out_ref[rows, :] = gated.astype(BF16)


def mix_kernel(gated_ref, weight_ref, out_ref):
    parts, _, width = gated_ref.shape
    joined = jnp.concatenate([gated_ref[part] for part in range(parts)], axis=1)
    for part in range(0, parts, 2):
        mixed = dot(joined, weight_ref[:, pl.ds(part * width, 2 * width)]).astype(BF16)
        out_ref[part] = mixed[:, :width]
        out_ref[part + 1] = mixed[:, width:]


def call(kernel, shape, scratch=(), flops=0):
    return pl.pallas_call(
        kernel,
        out_shape=jax.ShapeDtypeStruct(shape, BF16),
        scratch_shapes=list(scratch),
        compiler_params=pltpu.CompilerParams(vmem_limit_bytes=48 << 20),
        cost_estimate=pl.CostEstimate(flops=flops, bytes_accessed=2 << 20, transcendentals=0),
    )


def shards(values, inner_gate, outer_gate, filters, skip, w_out):
    parts = lax.axis_size("seq")
    ranks = lax.axis_size("chan")
    length, channels = values.shape
    groups = filters.shape[1]
    tiles = length // LANES
    count = channels // parts
    packed = call(
        pack_kernel,
        (parts, (count + 1) * tiles, LANES),
        [pltpu.VMEM((channels * tiles, LANES), F32), pltpu.VMEM((groups * tiles, LANES), F32)],
    )(values, inner_gate, filters)
    moved = lax.all_to_all(packed, "seq", split_axis=0, concat_axis=0, tiled=True)
    conv = call(
        conv_kernel,
        (parts, count * tiles, LANES),
        [
            pltpu.VMEM((ROWS, count * LANES), BF16),
            pltpu.VMEM((ROWS, LANES), BF16),
            pltpu.VMEM((2 * ROWS, count * LANES), BF16),
            pltpu.VMEM((2 * ROWS, count * LANES), BF16),
        ],
        flops=5 * 10**9,
    )(moved, *[jnp.asarray(table) for table in tables(ROWS)])
    conv = lax.all_to_all(conv, "seq", split_axis=0, concat_axis=0, tiled=True)
    gated = call(gate_kernel, (length, channels), [pltpu.VMEM((channels * tiles, LANES), F32)])(
        conv, values, inner_gate, outer_gate, skip[None, :]
    )
    shape = (ranks, length // ranks, channels)
    gated = lax.all_to_all(gated.reshape(shape), "chan", split_axis=0, concat_axis=0, tiled=True)
    mixed = call(mix_kernel, shape, flops=2 * length * channels * channels * ranks)(gated, w_out)
    mixed = lax.all_to_all(mixed, "chan", split_axis=0, concat_axis=0, tiled=True)
    return mixed.reshape(length, channels)


def solution(mesh):
    in_specs = (
        P("seq", "chan"),
        P("seq", "chan"),
        P("seq", "chan"),
        P("seq", "chan"),
        P("chan"),
        P(),
    )
    out_specs = P("seq", "chan")
    return jax.shard_map(shards, mesh=mesh, in_specs=in_specs, out_specs=out_specs, check_vma=False)
```

```python
import functools

import jax
import jax.numpy as jnp
import numpy as np
from jax import lax
from jax.experimental import pallas as pl
from jax.experimental.pallas import tpu as pltpu
from jax.sharding import PartitionSpec as P

F32 = jnp.float32
BF16 = jnp.bfloat16
MESH = pl.DeviceIdType.MESH
LANES = 128
STAGES = 2


def split_table(table):
    high = table.astype(jnp.bfloat16)
    low = (table - high.astype(np.float64)).astype(jnp.bfloat16)
    return high, low


@functools.lru_cache(maxsize=None)
def tables(rows):
    n = rows * LANES
    quarter = 4 * np.arange(rows, dtype=np.int64) + 1
    first = np.arange(rows, dtype=np.int64)
    angle = 2.0 * np.pi * ((quarter[:, None] * first[None, :]) % (4 * rows)) / (4 * rows)
    front = np.concatenate([np.cos(angle), -np.sin(angle)], axis=0)
    lane = np.arange(LANES, dtype=np.int64)
    angle = 2.0 * np.pi * (quarter[:, None] * lane[None, :]) / (4 * n)
    twist_real = np.cos(angle).astype(np.float32)
    twist_imag = (-np.sin(angle)).astype(np.float32)
    angle = 2.0 * np.pi * ((lane[:, None] * lane[None, :]) % LANES) / LANES
    cos, sin = np.cos(angle), np.sin(angle)
    mid = np.block([[cos, -sin], [sin, cos]])
    back = np.block([[cos, sin], [-sin, cos]])
    return (
        *split_table(front),
        *split_table(front.T / n),
        *split_table(mid),
        *split_table(back),
        twist_real,
        twist_imag,
    )


def halves(value):
    high = value.astype(BF16)
    return high, (value - high.astype(F32)).astype(BF16)


def dot(left, right):
    return jnp.dot(left, right, preferred_element_type=F32)


def dot3(left, right_high, right_low):
    left_high, left_low = halves(left)
    return dot(left_high, right_high) + (dot(left_high, right_low) + dot(left_low, right_high))


def wait_all(ref, sem):
    pltpu.make_async_copy(ref, ref, sem).wait()


def exchange(axis, me, size, send_ref, place_of, send_sem, recv_sem, prepare=None):
    def one(step, carry):
        other = lax.rem(me + step, size)
        if prepare is not None:
            prepare(other)
        pltpu.make_async_remote_copy(
            src_ref=send_ref.at[other],
            dst_ref=place_of(me),
            send_sem=send_sem,
            recv_sem=recv_sem,
            device_id={axis: other},
            device_id_type=MESH,
        ).start()
        return carry

    lax.fori_loop(1, size, one, 0)
    if prepare is not None:
        prepare(me)
    pltpu.make_async_copy(send_ref.at[me], place_of(me), recv_sem).start()


def layer_kernel(parts, ranks, *refs):
    (values_hbm, inner_hbm, outer_hbm, filters_ref, skip_ref, weight_hbm) = refs[:6]
    table_hbm = refs[6:16]
    out_ref = refs[16]
    (values_ref, inner_ref, outer_ref, weight_ref) = refs[17:21]
    table_refs = refs[21:31]
    (wide_ref, wide_filter_ref, data_ref, filter_ref, high_ref, low_ref, kernel_real, kernel_imag) = refs[31:39]
    (first_sends, first_recvs, second_sends, second_recvs) = (
        refs[39:41],
        refs[41:43],
        refs[43:45],
        refs[45:47],
    )
    (third_sends, third_recvs, fourth_sends) = refs[47:49], refs[49:51], refs[51:53]
    load_sems, send_sems, recv_sems = refs[53:56]
    (front_high, front_low, rear_high, rear_low, mid_high, mid_low, back_high, back_low, twist_real, twist_imag) = (
        table_refs
    )
    length, channels = values_ref.shape
    groups = filters_ref.shape[0]
    tiles = length // LANES
    rows_all = tiles * parts
    count = channels // parts
    share = count // STAGES
    chunk = min(256, rows_all)
    me = lax.axis_index("seq")
    rank = lax.axis_index("chan")

    pairs = [
        (values_hbm, values_ref),
        (inner_hbm, inner_ref),
        (outer_hbm, outer_ref),
        *zip(table_hbm, table_refs),
        (weight_hbm, weight_ref),
    ]
    loads = [
        pltpu.make_async_copy(source, target, load_sems.at[i])
        for i, (source, target) in enumerate(pairs)
    ]
    for load in loads:
        load.start()

    barrier = pltpu.get_barrier_semaphore()

    def greet(axis, place, size):
        def one(step, carry):
            other = lax.rem(place + step, size)
            pl.semaphore_signal(barrier, inc=1, device_id={axis: other}, device_id_type=MESH)
            return carry

        lax.fori_loop(1, size, one, 0)

    greet("seq", me, parts)
    greet("chan", rank, ranks)

    for tile in range(tiles):
        wide_filter_ref[pl.ds(tile, groups, stride=tiles), :] = filters_ref[
            :, pl.ds(tile * LANES, LANES)
        ].astype(F32)
    loads[0].wait()
    loads[1].wait()
    for tile in range(tiles):
        rows = pl.ds(tile * LANES, LANES)
        signal = inner_ref[rows, :].astype(F32) * values_ref[rows, :].astype(F32)
        wide_ref[pl.ds(tile, channels, stride=tiles), :] = signal.T
    own = share * tiles
    for part in range(parts):
        group = part * groups // parts
        first_sends[0][part, :tiles, :] = wide_filter_ref[pl.ds(group * tiles, tiles), :].astype(BF16)
        for stage in range(STAGES):
            offset = tiles if stage == 0 else 0
            first_sends[stage][part, pl.ds(offset, own), :] = wide_ref[
                pl.ds(part * count * tiles + stage * own, own), :
            ].astype(BF16)
    pl.semaphore_wait(barrier, parts + ranks - 2)
    for stage in range(STAGES):
        exchange(
            "seq",
            me,
            parts,
            first_sends[stage],
            lambda place, stage=stage: first_recvs[stage].at[place],
            send_sems.at[stage],
            recv_sems.at[stage],
        )
    for load in loads[3:13]:
        load.wait()

    def forward(columns, rows):
        return dot(front_high[rows, :], columns) + dot(front_low[rows, :], columns)

    def convolve(stage):
        moved_ref = first_recvs[stage]
        offset = tiles if stage == 0 else 0
        for part in range(parts):
            rows = pl.ds(part * tiles, tiles)
            for channel in range(share):
                data_ref[rows, pl.ds(channel * LANES, LANES)] = moved_ref[
                    part, pl.ds(offset + channel * tiles, tiles), :
                ]
            if stage == 0:
                filter_ref[rows, :] = moved_ref[part, :tiles, :]

        def chunk_step(step, carry):
            start = pl.multiple_of(step * chunk, chunk)
            real_rows = pl.ds(start, chunk)
            imag_rows = pl.ds(pl.multiple_of(start + rows_all, chunk), chunk)
            turn_real, turn_imag = twist_real[real_rows, :], twist_imag[real_rows, :]

            def spectrum(real, imag):
                turned = jnp.concatenate(
                    [real * turn_real - imag * turn_imag, real * turn_imag + imag * turn_real], axis=1
                )
                both = dot3(turned, mid_high[...], mid_low[...])
                return both[:, :LANES], both[:, LANES:]

            if stage == 0:
                kernel = filter_ref[...]
                kernel_real[real_rows, :], kernel_imag[real_rows, :] = spectrum(
                    forward(kernel, real_rows), forward(kernel, imag_rows)
                )
            data = data_ref[...]
            all_real, all_imag = forward(data, real_rows), forward(data, imag_rows)
            for channel in range(share):
                lanes = slice(channel * LANES, (channel + 1) * LANES)
                real, imag = spectrum(all_real[:, lanes], all_imag[:, lanes])
                product = jnp.concatenate(
                    [
                        real * kernel_real[real_rows, :] - imag * kernel_imag[real_rows, :],
                        real * kernel_imag[real_rows, :] + imag * kernel_real[real_rows, :],
                    ],
                    axis=1,
                )
                both = dot3(product, back_high[...], back_low[...])
                real, imag = both[:, :LANES], both[:, LANES:]
                high, low = halves(real * turn_real + imag * turn_imag)
                high_ref[real_rows, lanes], low_ref[real_rows, lanes] = high, low
                high, low = halves(imag * turn_real - real * turn_imag)
                high_ref[imag_rows, lanes], low_ref[imag_rows, lanes] = high, low
            return carry

        lax.fori_loop(0, rows_all // chunk, chunk_step, 0)

        def rear_step(step, carry):
            rows = pl.ds(pl.multiple_of(step * chunk, chunk), chunk)
            high, low = high_ref[...], low_ref[...]
            result = dot(rear_high[rows, :], high) + (
                dot(rear_low[rows, :], high) + dot(rear_high[rows, :], low)
            )
            result = result.astype(BF16)
            several = chunk // tiles
            for channel in range(share):
                second_sends[stage][pl.ds(step * several, several), pl.ds(channel * tiles, tiles), :] = (
                    result[:, channel * LANES : (channel + 1) * LANES].reshape(several, tiles, LANES)
                )
            return carry

        lax.fori_loop(0, rows_all // chunk, rear_step, 0)

    for stage in range(STAGES):
        wait_all(first_recvs[stage], recv_sems.at[stage])
        convolve(stage)
        exchange(
            "seq",
            me,
            parts,
            second_sends[stage],
            lambda place, stage=stage: second_recvs[stage].at[place],
            send_sems.at[STAGES + stage],
            recv_sems.at[STAGES + stage],
        )
    loads[2].wait()
    loads[13].wait()
    for stage in range(STAGES):
        wait_all(second_recvs[stage], recv_sems.at[STAGES + stage])
        for part in range(parts):
            wide_ref[pl.ds((part * count + stage * share) * tiles, own), :] = second_recvs[stage][
                part
            ].astype(F32)

    block = tiles // (ranks * STAGES)
    for stage in range(STAGES):

        def gate(other, stage=stage):
            for i in range(block):
                tile = (other * STAGES + stage) * block + i
                rows = pl.ds(pl.multiple_of(tile * LANES, LANES), LANES)
                conv = wide_ref[pl.ds(tile, channels, stride=tiles), :].T
                signal = inner_ref[rows, :].astype(F32) * values_ref[rows, :].astype(F32)
                signal = signal.astype(BF16).astype(F32)
                gated = outer_ref[rows, :].astype(F32) * (conv + skip_ref[...] * signal)
                third_sends[stage][other, pl.ds(i * LANES, LANES), :] = gated.astype(BF16)

        exchange(
            "chan",
            rank,
            ranks,
            third_sends[stage],
            lambda place, stage=stage: third_recvs[stage].at[place],
            send_sems.at[2 * STAGES + stage],
            recv_sems.at[2 * STAGES + stage],
            gate,
        )

    for stage in range(STAGES):
        wait_all(third_recvs[stage], recv_sems.at[2 * STAGES + stage])
        joined = jnp.concatenate([third_recvs[stage][other] for other in range(ranks)], axis=1)
        for other in range(0, ranks, 2):
            mixed = dot(joined, weight_ref[:, pl.ds(other * channels, 2 * channels)]).astype(BF16)
            fourth_sends[stage][other] = mixed[:, :channels]
            fourth_sends[stage][other + 1] = mixed[:, channels:]
        exchange(
            "chan",
            rank,
            ranks,
            fourth_sends[stage],
            lambda place, stage=stage: out_ref.at[place, pl.ds(stage * block * LANES, block * LANES)],
            send_sems.at[3 * STAGES + stage],
            recv_sems.at[3 * STAGES + stage],
        )
    for stage in range(STAGES):
        wait_all(
            out_ref.at[:, pl.ds(stage * block * LANES, block * LANES)], recv_sems.at[3 * STAGES + stage]
        )
    for phase, (refs_of, size) in enumerate(
        [(first_sends, parts), (second_sends, parts), (third_sends, ranks), (fourth_sends, ranks)]
    ):
        for stage in range(STAGES):
            wait_all(refs_of[stage].at[pl.ds(0, size - 1)], send_sems.at[phase * STAGES + stage])


def shards(values, inner_gate, outer_gate, filters, skip, w_out):
    parts = lax.axis_size("seq")
    ranks = lax.axis_size("chan")
    length, channels = values.shape
    groups = filters.shape[1]
    tiles = length // LANES
    rows_all = tiles * parts
    count = channels // parts
    share = count // STAGES
    own = share * tiles
    positions = length // ranks
    constants = [jnp.asarray(table) for table in tables(rows_all)]
    any_spec = pl.BlockSpec(memory_space=pl.ANY)
    vmem_spec = pl.BlockSpec(memory_space=pltpu.VMEM)
    local = pltpu.VMEM((length, channels), BF16)
    first = [pltpu.VMEM((parts, own + (tiles if s == 0 else 0), LANES), BF16) for s in range(STAGES)]
    second = [pltpu.VMEM((parts, own, LANES), BF16)] * STAGES
    third = [pltpu.VMEM((ranks, positions // STAGES, channels), BF16)] * STAGES
    mixed = pl.pallas_call(
        functools.partial(layer_kernel, parts, ranks),
        out_shape=jax.ShapeDtypeStruct((ranks, positions, channels), BF16),
        in_specs=[any_spec] * 3 + [vmem_spec] * 2 + [any_spec] * 11,
        out_specs=any_spec,
        scratch_shapes=[
            local,
            local,
            local,
            pltpu.VMEM(w_out.shape, BF16),
            *[pltpu.VMEM(table.shape, table.dtype) for table in constants],
            pltpu.VMEM((channels * tiles, LANES), F32),
            pltpu.VMEM((groups * tiles, LANES), F32),
            pltpu.VMEM((rows_all, share * LANES), BF16),
            pltpu.VMEM((rows_all, LANES), BF16),
            pltpu.VMEM((2 * rows_all, share * LANES), BF16),
            pltpu.VMEM((2 * rows_all, share * LANES), BF16),
            pltpu.VMEM((rows_all, LANES), F32),
            pltpu.VMEM((rows_all, LANES), F32),
            *first,
            *first,
            *second,
            *second,
            *third,
            *third,
            *third,
            pltpu.SemaphoreType.DMA((14,)),
            pltpu.SemaphoreType.DMA((4 * STAGES,)),
            pltpu.SemaphoreType.DMA((4 * STAGES,)),
        ],
        compiler_params=pltpu.CompilerParams(
            collective_id=0, has_side_effects=True, vmem_limit_bytes=48 << 20
        ),
    )(values, inner_gate, outer_gate, filters.T, skip[None, :], w_out, *constants)
    return mixed.reshape(length, channels)


def solution(mesh):
    in_specs = (
        P("seq", "chan"),
        P("seq", "chan"),
        P("seq", "chan"),
        P("seq", "chan"),
        P("chan"),
        P(),
    )
    out_specs = P("seq", "chan")
    return jax.shard_map(shards, mesh=mesh, in_specs=in_specs, out_specs=out_specs, check_vma=False)
```

```python
import functools

import jax
import jax.numpy as jnp
import numpy as np
from jax import lax
from jax.experimental import pallas as pl
from jax.experimental.pallas import tpu as pltpu
from jax.sharding import PartitionSpec as P

F32 = jnp.float32
BF16 = jnp.bfloat16
MESH = pl.DeviceIdType.MESH
LANES = 128
STAGES = 2


def split_table(table):
    high = table.astype(jnp.bfloat16)
    low = (table - high.astype(np.float64)).astype(jnp.bfloat16)
    return high, low


@functools.lru_cache(maxsize=None)
def tables(rows):
    n = rows * LANES
    quarter = 4 * np.arange(rows, dtype=np.int64) + 1
    first = np.arange(rows, dtype=np.int64)
    angle = 2.0 * np.pi * ((quarter[:, None] * first[None, :]) % (4 * rows)) / (4 * rows)
    front = np.concatenate([np.cos(angle), -np.sin(angle)], axis=0)
    lane = np.arange(LANES, dtype=np.int64)
    angle = 2.0 * np.pi * (quarter[:, None] * lane[None, :]) / (4 * n)
    twist_real = np.cos(angle).astype(np.float32)
    twist_imag = (-np.sin(angle)).astype(np.float32)
    angle = 2.0 * np.pi * ((lane[:, None] * lane[None, :]) % LANES) / LANES
    cos, sin = np.cos(angle), np.sin(angle)
    mid = np.block([[cos, -sin], [sin, cos]])
    back = np.block([[cos, sin], [-sin, cos]])
    return (
        *split_table(front),
        *split_table(front.T / n),
        *split_table(mid),
        *split_table(back),
        twist_real,
        twist_imag,
    )


def halves(value):
    high = value.astype(BF16)
    return high, (value - high.astype(F32)).astype(BF16)


def dot(left, right):
    return jnp.dot(left, right, preferred_element_type=F32)


def dot3(left, right_high, right_low):
    left_high, left_low = halves(left)
    return dot(left_high, right_high) + (dot(left_high, right_low) + dot(left_low, right_high))


def wait_all(ref, sem):
    pltpu.make_async_copy(ref, ref, sem).wait()


def exchange(axis, me, size, send_ref, place_of, send_sem, recv_sem, prepare=None):
    def one(step, carry):
        other = lax.rem(me + step, size)
        if prepare is not None:
            prepare(other)
        pltpu.make_async_remote_copy(
            src_ref=send_ref.at[other],
            dst_ref=place_of(me),
            send_sem=send_sem,
            recv_sem=recv_sem,
            device_id={axis: other},
            device_id_type=MESH,
        ).start()
        return carry

    lax.fori_loop(1, size, one, 0)
    if prepare is not None:
        prepare(me)
    pltpu.make_async_copy(send_ref.at[me], place_of(me), recv_sem).start()


def layer_kernel(parts, ranks, *refs):
    (values_hbm, inner_hbm, outer_hbm, filters_ref, skip_ref, weight_hbm) = refs[:6]
    table_hbm = refs[6:16]
    out_ref = refs[16]
    (values_ref, inner_ref, outer_ref, weight_ref) = refs[17:21]
    table_refs = refs[21:31]
    (wide_ref, wide_filter_ref, data_ref, filter_ref, high_ref, low_ref, kernel_real, kernel_imag) = refs[31:39]
    (first_sends, first_recvs, second_sends, second_recvs) = (
        refs[39:41],
        refs[41:43],
        refs[43:45],
        refs[45:47],
    )
    (third_sends, third_recvs, fourth_sends) = refs[47:49], refs[49:51], refs[51:53]
    load_sems, send_sems, recv_sems, filter_send, filter_recv = refs[53:58]
    filter_sends, filter_moved = refs[58:60]
    (front_high, front_low, rear_high, rear_low, mid_high, mid_low, back_high, back_low, twist_real, twist_imag) = (
        table_refs
    )
    length, channels = values_ref.shape
    groups = filters_ref.shape[0]
    tiles = length // LANES
    rows_all = tiles * parts
    count = channels // parts
    share = count // STAGES
    chunk = min(256, rows_all)
    me = lax.axis_index("seq")
    rank = lax.axis_index("chan")

    pairs = [
        (values_hbm, values_ref),
        (inner_hbm, inner_ref),
        (outer_hbm, outer_ref),
        *zip(table_hbm, table_refs),
        (weight_hbm, weight_ref),
    ]
    loads = [
        pltpu.make_async_copy(source, target, load_sems.at[i])
        for i, (source, target) in enumerate(pairs)
    ]
    for load in loads:
        load.start()

    barrier = pltpu.get_barrier_semaphore()

    def greet(axis, place, size):
        def one(step, carry):
            other = lax.rem(place + step, size)
            pl.semaphore_signal(barrier, inc=1, device_id={axis: other}, device_id_type=MESH)
            return carry

        lax.fori_loop(1, size, one, 0)

    greet("chan", rank, ranks)
    greet("seq", me, parts)

    for tile in range(tiles):
        wide_filter_ref[pl.ds(tile, groups, stride=tiles), :] = filters_ref[
            :, pl.ds(tile * LANES, LANES)
        ].astype(F32)
    loads[0].wait()
    loads[1].wait()
    for tile in range(tiles):
        rows = pl.ds(tile * LANES, LANES)
        signal = inner_ref[rows, :].astype(F32) * values_ref[rows, :].astype(F32)
        wide_ref[pl.ds(tile, channels, stride=tiles), :] = signal.T
    own = share * tiles
    filter_sends[...] = wide_filter_ref[...].astype(BF16).reshape(groups, tiles, LANES)
    for part in range(parts):
        for stage in range(STAGES):
            first_sends[stage][part] = wide_ref[
                pl.ds(part * count * tiles + stage * own, own), :
            ].astype(BF16)
    pl.semaphore_wait(barrier, parts + ranks - 2)

    sharers = parts // groups
    each = parts // sharers
    kind = lax.rem(me, sharers)

    def send_filter(group, carry):
        pltpu.make_async_remote_copy(
            src_ref=filter_sends.at[group],
            dst_ref=filter_moved.at[kind * each + me // sharers],
            send_sem=filter_send.at[0],
            recv_sem=filter_recv.at[0],
            device_id={"seq": group * sharers + lax.rem(kind + 1, sharers)},
            device_id_type=MESH,
        ).start()
        return carry

    lax.fori_loop(0, groups, send_filter, 0)

    def send_signal(stage):
        exchange(
            "seq",
            me,
            parts,
            first_sends[stage],
            lambda place: first_recvs[stage].at[place],
            send_sems.at[stage],
            recv_sems.at[stage],
        )

    send_signal(0)
    wait_all(filter_sends, filter_recv.at[0])
    held = filter_moved.at[pl.ds(lax.rem(kind + sharers - 1, sharers) * each, each)]

    def pass_filter(step, carry):
        pltpu.make_async_remote_copy(
            src_ref=held,
            dst_ref=held,
            send_sem=filter_send.at[1],
            recv_sem=filter_recv.at[1],
            device_id={"seq": me - kind + lax.rem(kind + step, sharers)},
            device_id_type=MESH,
        ).start()
        return carry

    lax.fori_loop(1, sharers, pass_filter, 0)
    for stage in range(1, STAGES):
        send_signal(stage)
    for load in loads[3:13]:
        load.wait()

    def forward(columns, rows):
        return dot(front_high[rows, :], columns) + dot(front_low[rows, :], columns)

    def chunk_rows(step):
        start = pl.multiple_of(step * chunk, chunk)
        return pl.ds(start, chunk), pl.ds(pl.multiple_of(start + rows_all, chunk), chunk)

    def spectrum(real, imag, turn_real, turn_imag):
        turned = jnp.concatenate(
            [real * turn_real - imag * turn_imag, real * turn_imag + imag * turn_real], axis=1
        )
        both = dot3(turned, mid_high[...], mid_low[...])
        return both[:, :LANES], both[:, LANES:]

    def filter_step(step, carry):
        real_rows, imag_rows = chunk_rows(step)
        kernel = filter_ref[...]
        kernel_real[real_rows, :], kernel_imag[real_rows, :] = spectrum(
            forward(kernel, real_rows),
            forward(kernel, imag_rows),
            twist_real[real_rows, :],
            twist_imag[real_rows, :],
        )
        return carry

    wait_all(filter_moved.at[pl.ds(0, parts - each)], filter_recv.at[1])
    for part in range(parts):
        filter_ref[pl.ds(part * tiles, tiles), :] = filter_moved[part % sharers * each + part // sharers]
    lax.fori_loop(0, rows_all // chunk, filter_step, 0)

    def convolve(stage):
        moved_ref = first_recvs[stage]
        for part in range(parts):
            rows = pl.ds(part * tiles, tiles)
            for channel in range(share):
                data_ref[rows, pl.ds(channel * LANES, LANES)] = moved_ref[
                    part, pl.ds(channel * tiles, tiles), :
                ]

        def chunk_step(step, carry):
            real_rows, imag_rows = chunk_rows(step)
            turn_real, turn_imag = twist_real[real_rows, :], twist_imag[real_rows, :]
            data = data_ref[...]
            all_real, all_imag = forward(data, real_rows), forward(data, imag_rows)
            for channel in range(share):
                lanes = slice(channel * LANES, (channel + 1) * LANES)
                real, imag = spectrum(all_real[:, lanes], all_imag[:, lanes], turn_real, turn_imag)
                product = jnp.concatenate(
                    [
                        real * kernel_real[real_rows, :] - imag * kernel_imag[real_rows, :],
                        real * kernel_imag[real_rows, :] + imag * kernel_real[real_rows, :],
                    ],
                    axis=1,
                )
                both = dot3(product, back_high[...], back_low[...])
                real, imag = both[:, :LANES], both[:, LANES:]
                high, low = halves(real * turn_real + imag * turn_imag)
                high_ref[real_rows, lanes], low_ref[real_rows, lanes] = high, low
                high, low = halves(imag * turn_real - real * turn_imag)
                high_ref[imag_rows, lanes], low_ref[imag_rows, lanes] = high, low
            return carry

        lax.fori_loop(0, rows_all // chunk, chunk_step, 0)

        def rear_step(step, carry):
            rows = pl.ds(pl.multiple_of(step * chunk, chunk), chunk)
            high, low = high_ref[...], low_ref[...]
            result = dot(rear_high[rows, :], high) + (
                dot(rear_low[rows, :], high) + dot(rear_high[rows, :], low)
            )
            result = result.astype(BF16)
            several = chunk // tiles
            for channel in range(share):
                second_sends[stage][pl.ds(step * several, several), pl.ds(channel * tiles, tiles), :] = (
                    result[:, channel * LANES : (channel + 1) * LANES].reshape(several, tiles, LANES)
                )
            return carry

        lax.fori_loop(0, rows_all // chunk, rear_step, 0)

    for stage in range(STAGES):
        wait_all(first_recvs[stage], recv_sems.at[stage])
        convolve(stage)
        exchange(
            "seq",
            me,
            parts,
            second_sends[stage],
            lambda place, stage=stage: second_recvs[stage].at[place],
            send_sems.at[STAGES + stage],
            recv_sems.at[STAGES + stage],
        )
    loads[2].wait()
    loads[13].wait()
    for stage in range(STAGES):
        wait_all(second_recvs[stage], recv_sems.at[STAGES + stage])
        for part in range(parts):
            wide_ref[pl.ds((part * count + stage * share) * tiles, own), :] = second_recvs[stage][
                part
            ].astype(F32)

    block = tiles // (ranks * STAGES)
    for stage in range(STAGES):

        def gate(other, stage=stage):
            for i in range(block):
                tile = (other * STAGES + stage) * block + i
                rows = pl.ds(pl.multiple_of(tile * LANES, LANES), LANES)
                conv = wide_ref[pl.ds(tile, channels, stride=tiles), :].T
                signal = inner_ref[rows, :].astype(F32) * values_ref[rows, :].astype(F32)
                signal = signal.astype(BF16).astype(F32)
                gated = outer_ref[rows, :].astype(F32) * (conv + skip_ref[...] * signal)
                third_sends[stage][other, pl.ds(i * LANES, LANES), :] = gated.astype(BF16)

        exchange(
            "chan",
            rank,
            ranks,
            third_sends[stage],
            lambda place, stage=stage: third_recvs[stage].at[place],
            send_sems.at[2 * STAGES + stage],
            recv_sems.at[2 * STAGES + stage],
            gate,
        )

    for stage in range(STAGES):
        wait_all(third_recvs[stage], recv_sems.at[2 * STAGES + stage])
        joined = jnp.concatenate([third_recvs[stage][other] for other in range(ranks)], axis=1)
        for other in range(0, ranks, 2):
            mixed = dot(joined, weight_ref[:, pl.ds(other * channels, 2 * channels)]).astype(BF16)
            fourth_sends[stage][other] = mixed[:, :channels]
            fourth_sends[stage][other + 1] = mixed[:, channels:]
        exchange(
            "chan",
            rank,
            ranks,
            fourth_sends[stage],
            lambda place, stage=stage: out_ref.at[place, pl.ds(stage * block * LANES, block * LANES)],
            send_sems.at[3 * STAGES + stage],
            recv_sems.at[3 * STAGES + stage],
        )
    for stage in range(STAGES):
        wait_all(
            out_ref.at[:, pl.ds(stage * block * LANES, block * LANES)], recv_sems.at[3 * STAGES + stage]
        )
    wait_all(filter_sends, filter_send.at[0])
    wait_all(filter_moved.at[pl.ds(0, parts - each)], filter_send.at[1])
    for phase, (refs_of, size) in enumerate(
        [(first_sends, parts), (second_sends, parts), (third_sends, ranks), (fourth_sends, ranks)]
    ):
        for stage in range(STAGES):
            wait_all(refs_of[stage].at[pl.ds(0, size - 1)], send_sems.at[phase * STAGES + stage])


def shards(values, inner_gate, outer_gate, filters, skip, w_out):
    parts = lax.axis_size("seq")
    ranks = lax.axis_size("chan")
    length, channels = values.shape
    groups = filters.shape[1]
    tiles = length // LANES
    rows_all = tiles * parts
    count = channels // parts
    share = count // STAGES
    own = share * tiles
    positions = length // ranks
    constants = [jnp.asarray(table) for table in tables(rows_all)]
    hbm_spec = pl.BlockSpec(memory_space=pltpu.HBM)
    vmem_spec = pl.BlockSpec(memory_space=pltpu.VMEM)
    local = pltpu.VMEM((length, channels), BF16)
    moved = [pltpu.VMEM((parts, own, LANES), BF16)] * STAGES
    third = [pltpu.VMEM((ranks, positions // STAGES, channels), BF16)] * STAGES
    mixed = pl.pallas_call(
        functools.partial(layer_kernel, parts, ranks),
        out_shape=jax.ShapeDtypeStruct((ranks, positions, channels), BF16),
        in_specs=[hbm_spec] * 3 + [vmem_spec] * 2 + [hbm_spec] * 11,
        out_specs=hbm_spec,
        scratch_shapes=[
            local,
            local,
            local,
            pltpu.VMEM(w_out.shape, BF16),
            *[pltpu.VMEM(table.shape, table.dtype) for table in constants],
            pltpu.VMEM((channels * tiles, LANES), F32),
            pltpu.VMEM((groups * tiles, LANES), F32),
            pltpu.VMEM((rows_all, share * LANES), BF16),
            pltpu.VMEM((rows_all, LANES), BF16),
            pltpu.VMEM((2 * rows_all, share * LANES), BF16),
            pltpu.VMEM((2 * rows_all, share * LANES), BF16),
            pltpu.VMEM((rows_all, LANES), F32),
            pltpu.VMEM((rows_all, LANES), F32),
            *moved * 4,
            *third,
            *third,
            *third,
            pltpu.SemaphoreType.DMA((14,)),
            pltpu.SemaphoreType.DMA((4 * STAGES,)),
            pltpu.SemaphoreType.DMA((4 * STAGES,)),
            pltpu.SemaphoreType.DMA((2,)),
            pltpu.SemaphoreType.DMA((2,)),
            pltpu.VMEM((groups, tiles, LANES), BF16),
            pltpu.VMEM((parts, tiles, LANES), BF16),
        ],
        compiler_params=pltpu.CompilerParams(
            collective_id=0, has_side_effects=True, vmem_limit_bytes=56 << 20
        ),
    )(values, inner_gate, outer_gate, filters.T, skip[None, :], w_out, *constants)
    return mixed.reshape(length, channels)


def solution(mesh):
    in_specs = (
        P("seq", "chan"),
        P("seq", "chan"),
        P("seq", "chan"),
        P("seq", "chan"),
        P("chan"),
        P(),
    )
    out_specs = P("seq", "chan")
    return jax.shard_map(shards, mesh=mesh, in_specs=in_specs, out_specs=out_specs, check_vma=False)
```

```python
import functools

import jax
import jax.numpy as jnp
import numpy as np
from jax import lax
from jax.experimental import pallas as pl
from jax.experimental.pallas import tpu as pltpu
from jax.sharding import PartitionSpec as P

F32 = jnp.float32
BF16 = jnp.bfloat16
MESH = pl.DeviceIdType.MESH
LANES = 128
STAGES = 2


def split_table(table):
    high = table.astype(jnp.bfloat16)
    low = (table - high.astype(np.float64)).astype(jnp.bfloat16)
    return high, low


@functools.lru_cache(maxsize=None)
def tables(rows):
    n = rows * LANES
    quarter = 4 * np.arange(rows, dtype=np.int64) + 1
    first = np.arange(rows, dtype=np.int64)
    angle = 2.0 * np.pi * ((quarter[:, None] * first[None, :]) % (4 * rows)) / (4 * rows)
    front = np.concatenate([np.cos(angle), -np.sin(angle)], axis=0)
    lane = np.arange(LANES, dtype=np.int64)
    angle = 2.0 * np.pi * (quarter[:, None] * lane[None, :]) / (4 * n)
    twist_real = np.cos(angle).astype(np.float32)
    twist_imag = (-np.sin(angle)).astype(np.float32)
    angle = 2.0 * np.pi * ((lane[:, None] * lane[None, :]) % LANES) / LANES
    cos, sin = np.cos(angle), np.sin(angle)
    mid = np.block([[cos, -sin], [sin, cos]])
    back = np.block([[cos, sin], [-sin, cos]])
    front_high, front_low = split_table(front)
    rear_high, rear_low = split_table(front.T / n)
    mid_high, mid_low = split_table(mid)
    back_high, back_low = split_table(back)
    return (
        np.concatenate([front_high, front_low], axis=1),
        np.concatenate([rear_high, rear_high, rear_low], axis=1),
        np.concatenate([mid_high, mid_high, mid_low], axis=0),
        np.concatenate([back_high, back_high, back_low], axis=0),
        twist_real,
        twist_imag,
    )


def halves(value):
    high = value.astype(BF16)
    return high, (value - high.astype(F32)).astype(BF16)


def dot(left, right):
    return jnp.dot(left, right, preferred_element_type=F32)


def dot3(left, table):
    high, low = halves(left)
    return dot(jnp.concatenate([high, low, high], axis=1), table)


def wait_all(ref, sem):
    pltpu.make_async_copy(ref, ref, sem).wait()


def exchange(axis, me, size, send_ref, place_of, send_sem, recv_sem, prepare=None):
    def one(step, carry):
        other = lax.rem(me + step, size)
        if prepare is not None:
            prepare(other)
        pltpu.make_async_remote_copy(
            src_ref=send_ref.at[other],
            dst_ref=place_of(me),
            send_sem=send_sem,
            recv_sem=recv_sem,
            device_id={axis: other},
            device_id_type=MESH,
        ).start()
        return carry

    lax.fori_loop(1, size, one, 0)
    if prepare is not None:
        prepare(me)
    pltpu.make_async_copy(send_ref.at[me], place_of(me), recv_sem).start()


def layer_kernel(parts, ranks, *refs):
    (values_hbm, inner_hbm, outer_hbm, filters_ref, skip_ref, weight_hbm) = refs[:6]
    table_hbm = refs[6:12]
    out_ref = refs[12]
    (values_ref, inner_ref, outer_ref, weight_ref) = refs[13:17]
    table_refs = refs[17:23]
    (wide_ref, wide_filter_ref, data_ref, filter_ref, split_ref, kernel_real, kernel_imag) = refs[23:30]
    (first_sends, first_recvs, second_sends, second_recvs) = (
        refs[30:32],
        refs[32:34],
        refs[34:36],
        refs[36:38],
    )
    (third_sends, third_recvs, fourth_sends) = refs[38:40], refs[40:42], refs[42:44]
    load_sems, send_sems, recv_sems, filter_send, filter_recv = refs[44:49]
    filter_sends, filter_moved = refs[49:51]
    front_table, rear_table, mid_table, back_table, twist_real, twist_imag = table_refs
    length, channels = values_ref.shape
    groups = filters_ref.shape[0]
    tiles = length // LANES
    rows_all = tiles * parts
    count = channels // parts
    share = count // STAGES
    chunk = min(512, rows_all)
    me = lax.axis_index("seq")
    rank = lax.axis_index("chan")

    pairs = [
        (values_hbm, values_ref),
        (inner_hbm, inner_ref),
        (outer_hbm, outer_ref),
        *zip(table_hbm, table_refs),
        (weight_hbm, weight_ref),
    ]
    loads = [
        pltpu.make_async_copy(source, target, load_sems.at[i])
        for i, (source, target) in enumerate(pairs)
    ]
    for load in loads:
        load.start()

    barrier = pltpu.get_barrier_semaphore()

    def greet(axis, place, size):
        def one(step, carry):
            other = lax.rem(place + step, size)
            pl.semaphore_signal(barrier, inc=1, device_id={axis: other}, device_id_type=MESH)
            return carry

        lax.fori_loop(1, size, one, 0)

    greet("chan", rank, ranks)
    greet("seq", me, parts)

    for tile in range(tiles):
        wide_filter_ref[pl.ds(tile, groups, stride=tiles), :] = filters_ref[
            :, pl.ds(tile * LANES, LANES)
        ].astype(F32)
    loads[0].wait()
    loads[1].wait()
    for tile in range(tiles):
        rows = pl.ds(tile * LANES, LANES)
        signal = inner_ref[rows, :].astype(F32) * values_ref[rows, :].astype(F32)
        wide_ref[pl.ds(tile, channels, stride=tiles), :] = signal.T
    own = share * tiles
    filter_sends[...] = wide_filter_ref[...].astype(BF16).reshape(groups, tiles, LANES)
    for part in range(parts):
        for stage in range(STAGES):
            first_sends[stage][part] = wide_ref[
                pl.ds(part * count * tiles + stage * own, own), :
            ].astype(BF16)
    pl.semaphore_wait(barrier, parts + ranks - 2)

    sharers = parts // groups
    each = parts // sharers
    kind = lax.rem(me, sharers)

    def send_filter(group, carry):
        pltpu.make_async_remote_copy(
            src_ref=filter_sends.at[group],
            dst_ref=filter_moved.at[kind * each + me // sharers],
            send_sem=filter_send.at[0],
            recv_sem=filter_recv.at[0],
            device_id={"seq": group * sharers + lax.rem(kind + 1, sharers)},
            device_id_type=MESH,
        ).start()
        return carry

    lax.fori_loop(0, groups, send_filter, 0)

    def send_signal(stage):
        exchange(
            "seq",
            me,
            parts,
            first_sends[stage],
            lambda place: first_recvs[stage].at[place],
            send_sems.at[stage],
            recv_sems.at[stage],
        )

    send_signal(0)
    wait_all(filter_sends, filter_recv.at[0])
    held = filter_moved.at[pl.ds(lax.rem(kind + sharers - 1, sharers) * each, each)]

    def pass_filter(step, carry):
        pltpu.make_async_remote_copy(
            src_ref=held,
            dst_ref=held,
            send_sem=filter_send.at[1],
            recv_sem=filter_recv.at[1],
            device_id={"seq": me - kind + lax.rem(kind + step, sharers)},
            device_id_type=MESH,
        ).start()
        return carry

    lax.fori_loop(1, sharers, pass_filter, 0)
    for stage in range(1, STAGES):
        send_signal(stage)
    for load in loads[3:9]:
        load.wait()

    def forward(columns, rows):
        return dot(front_table[rows, :], columns)

    def chunk_rows(step):
        start = pl.multiple_of(step * chunk, chunk)
        return pl.ds(start, chunk), pl.ds(pl.multiple_of(start + rows_all, chunk), chunk)

    def spectrum(real, imag, turn_real, turn_imag):
        turned = jnp.concatenate(
            [real * turn_real - imag * turn_imag, real * turn_imag + imag * turn_real], axis=1
        )
        both = dot3(turned, mid_table[...])
        return both[:, :LANES], both[:, LANES:]

    def filter_step(step, carry):
        real_rows, imag_rows = chunk_rows(step)
        kernel = filter_ref[...]
        kernel_real[real_rows, :], kernel_imag[real_rows, :] = spectrum(
            forward(kernel, real_rows),
            forward(kernel, imag_rows),
            twist_real[real_rows, :],
            twist_imag[real_rows, :],
        )
        return carry

    wait_all(filter_moved.at[pl.ds(0, parts - each)], filter_recv.at[1])
    for part in range(parts):
        block_of = filter_moved[part % sharers * each + part // sharers]
        filter_ref[pl.ds(part * tiles, tiles), :] = block_of
        filter_ref[pl.ds(rows_all + part * tiles, tiles), :] = block_of
    lax.fori_loop(0, rows_all // chunk, filter_step, 0)

    def convolve(stage):
        moved_ref = first_recvs[stage]
        for part in range(parts):
            rows = pl.ds(part * tiles, tiles)
            for channel in range(share):
                lanes = pl.ds(channel * LANES, LANES)
                block_of = moved_ref[part, pl.ds(channel * tiles, tiles), :]
                data_ref[rows, lanes] = block_of
                data_ref[pl.ds(rows_all + part * tiles, tiles), lanes] = block_of

        def chunk_step(step, carry):
            real_rows, imag_rows = chunk_rows(step)
            turn_real, turn_imag = twist_real[real_rows, :], twist_imag[real_rows, :]
            data = data_ref[...]
            all_real, all_imag = forward(data, real_rows), forward(data, imag_rows)
            for channel in range(share):
                lanes = slice(channel * LANES, (channel + 1) * LANES)
                real, imag = spectrum(all_real[:, lanes], all_imag[:, lanes], turn_real, turn_imag)
                product = jnp.concatenate(
                    [
                        real * kernel_real[real_rows, :] - imag * kernel_imag[real_rows, :],
                        real * kernel_imag[real_rows, :] + imag * kernel_real[real_rows, :],
                    ],
                    axis=1,
                )
                both = dot3(product, back_table[...])
                real, imag = both[:, :LANES], both[:, LANES:]
                for rows, value in (
                    (real_rows, real * turn_real + imag * turn_imag),
                    (imag_rows, imag * turn_real - real * turn_imag),
                ):
                    high, low = halves(value)
                    split_ref[rows, lanes] = high
                    split_ref[pl.ds(rows.start + 2 * rows_all, chunk), lanes] = low
                    split_ref[pl.ds(rows.start + 4 * rows_all, chunk), lanes] = high
            return carry

        lax.fori_loop(0, rows_all // chunk, chunk_step, 0)

        def rear_step(step, carry):
            rows = pl.ds(pl.multiple_of(step * chunk, chunk), chunk)
            result = dot(rear_table[rows, :], split_ref[...]).astype(BF16)
            several = chunk // tiles
            for channel in range(share):
                second_sends[stage][pl.ds(step * several, several), pl.ds(channel * tiles, tiles), :] = (
                    result[:, channel * LANES : (channel + 1) * LANES].reshape(several, tiles, LANES)
                )
            return carry

        lax.fori_loop(0, rows_all // chunk, rear_step, 0)

    for stage in range(STAGES):
        wait_all(first_recvs[stage], recv_sems.at[stage])
        convolve(stage)
        exchange(
            "seq",
            me,
            parts,
            second_sends[stage],
            lambda place, stage=stage: second_recvs[stage].at[place],
            send_sems.at[STAGES + stage],
            recv_sems.at[STAGES + stage],
        )
    loads[2].wait()
    loads[9].wait()
    for stage in range(STAGES):
        wait_all(second_recvs[stage], recv_sems.at[STAGES + stage])
        for part in range(parts):
            wide_ref[pl.ds((part * count + stage * share) * tiles, own), :] = second_recvs[stage][
                part
            ].astype(F32)

    block = tiles // (ranks * STAGES)
    for stage in range(STAGES):

        def gate(other, stage=stage):
            for i in range(block):
                tile = (other * STAGES + stage) * block + i
                rows = pl.ds(pl.multiple_of(tile * LANES, LANES), LANES)
                conv = wide_ref[pl.ds(tile, channels, stride=tiles), :].T
                signal = inner_ref[rows, :].astype(F32) * values_ref[rows, :].astype(F32)
                signal = signal.astype(BF16).astype(F32)
                gated = outer_ref[rows, :].astype(F32) * (conv + skip_ref[...] * signal)
                third_sends[stage][other, pl.ds(i * LANES, LANES), :] = gated.astype(BF16)

        exchange(
            "chan",
            rank,
            ranks,
            third_sends[stage],
            lambda place, stage=stage: third_recvs[stage].at[place],
            send_sems.at[2 * STAGES + stage],
            recv_sems.at[2 * STAGES + stage],
            gate,
        )

    for stage in range(STAGES):
        wait_all(third_recvs[stage], recv_sems.at[2 * STAGES + stage])
        joined = jnp.concatenate([third_recvs[stage][other] for other in range(ranks)], axis=1)
        for other in range(0, ranks, 2):
            mixed = dot(joined, weight_ref[:, pl.ds(other * channels, 2 * channels)]).astype(BF16)
            fourth_sends[stage][other] = mixed[:, :channels]
            fourth_sends[stage][other + 1] = mixed[:, channels:]
        exchange(
            "chan",
            rank,
            ranks,
            fourth_sends[stage],
            lambda place, stage=stage: out_ref.at[place, pl.ds(stage * block * LANES, block * LANES)],
            send_sems.at[3 * STAGES + stage],
            recv_sems.at[3 * STAGES + stage],
        )
    for stage in range(STAGES):
        wait_all(
            out_ref.at[:, pl.ds(stage * block * LANES, block * LANES)], recv_sems.at[3 * STAGES + stage]
        )
    wait_all(filter_sends, filter_send.at[0])
    wait_all(filter_moved.at[pl.ds(0, parts - each)], filter_send.at[1])
    for phase, (refs_of, size) in enumerate(
        [(first_sends, parts), (second_sends, parts), (third_sends, ranks), (fourth_sends, ranks)]
    ):
        for stage in range(STAGES):
            wait_all(refs_of[stage].at[pl.ds(0, size - 1)], send_sems.at[phase * STAGES + stage])


def shards(values, inner_gate, outer_gate, filters, skip, w_out):
    parts = lax.axis_size("seq")
    ranks = lax.axis_size("chan")
    length, channels = values.shape
    groups = filters.shape[1]
    tiles = length // LANES
    rows_all = tiles * parts
    count = channels // parts
    share = count // STAGES
    own = share * tiles
    positions = length // ranks
    constants = [jnp.asarray(table) for table in tables(rows_all)]
    hbm_spec = pl.BlockSpec(memory_space=pltpu.HBM)
    vmem_spec = pl.BlockSpec(memory_space=pltpu.VMEM)
    local = pltpu.VMEM((length, channels), BF16)
    moved = [pltpu.VMEM((parts, own, LANES), BF16)] * STAGES
    third = [pltpu.VMEM((ranks, positions // STAGES, channels), BF16)] * STAGES
    mixed = pl.pallas_call(
        functools.partial(layer_kernel, parts, ranks),
        out_shape=jax.ShapeDtypeStruct((ranks, positions, channels), BF16),
        in_specs=[hbm_spec] * 3 + [vmem_spec] * 2 + [hbm_spec] * 7,
        out_specs=hbm_spec,
        scratch_shapes=[
            local,
            local,
            local,
            pltpu.VMEM(w_out.shape, BF16),
            *[pltpu.VMEM(table.shape, table.dtype) for table in constants],
            pltpu.VMEM((channels * tiles, LANES), F32),
            pltpu.VMEM((groups * tiles, LANES), F32),
            pltpu.VMEM((2 * rows_all, share * LANES), BF16),
            pltpu.VMEM((2 * rows_all, LANES), BF16),
            pltpu.VMEM((6 * rows_all, share * LANES), BF16),
            pltpu.VMEM((rows_all, LANES), F32),
            pltpu.VMEM((rows_all, LANES), F32),
            *moved * 4,
            *third,
            *third,
            *third,
            pltpu.SemaphoreType.DMA((10,)),
            pltpu.SemaphoreType.DMA((4 * STAGES,)),
            pltpu.SemaphoreType.DMA((4 * STAGES,)),
            pltpu.SemaphoreType.DMA((2,)),
            pltpu.SemaphoreType.DMA((2,)),
            pltpu.VMEM((groups, tiles, LANES), BF16),
            pltpu.VMEM((parts, tiles, LANES), BF16),
        ],
        compiler_params=pltpu.CompilerParams(
            collective_id=0, has_side_effects=True, vmem_limit_bytes=56 << 20
        ),
    )(values, inner_gate, outer_gate, filters.T, skip[None, :], w_out, *constants)
    return mixed.reshape(length, channels)


def solution(mesh):
    in_specs = (
        P("seq", "chan"),
        P("seq", "chan"),
        P("seq", "chan"),
        P("seq", "chan"),
        P("chan"),
        P(),
    )
    out_specs = P("seq", "chan")
    return jax.shard_map(shards, mesh=mesh, in_specs=in_specs, out_specs=out_specs, check_vma=False)
```
